32 devices in a mesh: groups: 2 (over x), span: 16 (over z, y, core).
Axes of the slice: x: 2, y: 2, z: 4, core: 2. Of those that a mesh axis runs over, the one named last changes fastest.
Arguments:
- queries: bfloat16 [8192, 1024], P(('groups', 'span')), parts along dimension 0, may hold values from -96 to 96
- keys: bfloat16 [8192, 1024], P(('groups', 'span')), parts along dimension 0, may hold values from -9 to 9
- values: bfloat16 [8192, 1024], P(('groups', 'span')), parts along dimension 0, may hold values from -6 to 6
- track: int32 [64, 16], P(('groups', 'span')), parts along dimension 0, may hold values 0 or 1
- out_weight: bfloat16 [1024, 1024], replicated, may hold values from -0.1875 to 0.1875
- grad_out: bfloat16 [8192, 1024], P(('groups', 'span')), parts along dimension 0, may hold values from -6 to 6
Outputs:
- query_grad: bfloat16 [8192, 1024], P(('groups', 'span')), parts along dimension 0
- key_grad: bfloat16 [8192, 1024], P(('groups', 'span')), parts along dimension 0
- value_grad: bfloat16 [8192, 1024], P(('groups', 'span')), parts along dimension 0
- weight_grad: float32 [2048, 1024], P(('groups', 'span')), parts along dimension 0
The draws below stay inside these ranges and needn't reach their ends.
There are 2 independent parts, one for each index of `groups`. The reference program is written for one: setup_inputs(seed, part) draws one part's arguments, and reference() takes and returns one part's arrays. A program takes and returns all parts, laid end to end along the dimension named above; an argument that names none is the same for every part. Nothing has to cross between parts.
All inputs are finite; a program needn't handle non-finite values. No bound on the sum of `track` on one device may be relied on, other than what follows from the above.
Results may differ from the reference program's by a relative error of at most 0.039.
Values may be sent and summed in bfloat16 or wider, within the bound.
A program may use at most 64 MiB of HBM per device.

```python
import jax
import jax.numpy as jnp
from jax import lax

D = 1024
HEADS = 16
BLOCK = 128
TOK_DEV = 256
WINDOW = 8
TOKENS = 4096
QBLOCKS = 32
MEMBLOCKS = 16
N_SPAN = 16


def shared_keys(key):
    base = jax.random.fold_in(key, 7)
    raw = jnp.clip(1.5 * jax.random.normal(base, (TOKENS, D), jnp.float32), -9.0, 9.0)
    return raw


def draw_keys(key, part):
    return shared_keys(key).astype(jnp.bfloat16)


def draw_queries(key, part):
    base = jax.random.fold_in(key, 11)
    raw = jnp.clip(1.5 * jax.random.normal(base, (TOKENS, D), jnp.float32), -9.0, 9.0)
    return raw.astype(jnp.bfloat16)


def touch_ends(values, key, smallest, top_value):
    longest = values.shape.index(max(values.shape))
    spots = []
    for shift in (0, 1):
        where = [jax.random.randint(jax.random.fold_in(key, axis), (), 0, length) for axis, length in enumerate(values.shape)]
        where[longest] = (where[longest] + shift) % values.shape[longest]
        spots.append(tuple(where))
    return values.at[spots[0]].set(smallest).at[spots[1]].set(top_value)


def shard_levels(rng, shape, pieces, low, largest):
    factor_of = 1.0
    for dim, parts in pieces:
        steps = jax.random.uniform(jax.random.fold_in(jax.random.fold_in(rng, 6), dim), (parts,), jnp.float32, low / len(pieces), largest / len(pieces))
        factor_of = factor_of * jnp.repeat(jnp.exp(steps), shape[dim] // parts).reshape((-1,) + (1,) * (len(shape) - 1 - dim))
    return factor_of


def noise(key, dims, width, reach, cuts=(), kind=jnp.bfloat16):
    values = jax.random.normal(key, dims, jnp.float32) * width
    if len(cuts) > 0:
        values = shard_levels(key, dims, cuts, -0.22, 0.18) * values
    return jnp.clip(values, min=-reach, max=reach).astype(kind)


def setup_inputs(seed: int = 0, part: int = 0) -> dict:
    streams_of = jax.random.split(jax.random.key(seed), 7)
    part_keys = jax.random.split(jax.random.fold_in(streams_of[6], part), 7)
    return {
        "queries": draw_queries(jax.random.fold_in(jax.random.fold_in(streams_of[6], part), 71), part),
        "keys": draw_keys(jax.random.fold_in(jax.random.fold_in(streams_of[6], part), 71), part),
        "values": noise(part_keys[2], (TOKENS, D), 1.0, 6.0, ((0, 16),)),
        "track": touch_ends((jax.random.randint(part_keys[3], (QBLOCKS, MEMBLOCKS), 0, 2) < 1).astype(jnp.int32), jax.random.fold_in(part_keys[3], 1), 0, 1),
        "out_weight": noise(streams_of[4], (D, D), D ** -0.5, 0.1875),
        "grad_out": noise(part_keys[5], (TOKENS, D), 1.0, 6.0, ((0, 16),)),
    }


def head_grads(query_h, key_h, value_h, grad_h, allowed, local_count):
    scale = query_h.shape[-1] ** -0.5
    scores = jnp.einsum('rd,kd->rk', query_h.astype(jnp.float32), key_h.astype(jnp.float32)) * scale
    scores = jnp.where(allowed, scores, jnp.float32(-1e30))
    top = jnp.max(scores, axis=-1, keepdims=True)
    expo = jnp.exp(scores - top)
    probs = expo / jnp.sum(expo, axis=-1, keepdims=True)
    probs_low = probs.astype(jnp.bfloat16)
    attn = jnp.einsum('rk,kd->rd', probs_low.astype(jnp.float32), value_h.astype(jnp.float32)).astype(jnp.bfloat16)
    delta = jnp.sum(grad_h.astype(jnp.float32) * attn.astype(jnp.float32), axis=-1)
    dprob = jnp.einsum('rd,kd->rk', grad_h.astype(jnp.float32), value_h.astype(jnp.float32))
    dscore = (probs * (dprob - delta[:, None])).astype(jnp.bfloat16)
    query_g = (jnp.einsum('rk,kd->rd', dscore.astype(jnp.float32), key_h.astype(jnp.float32)) * scale).astype(jnp.bfloat16)
    key_g = (jnp.einsum('rk,rd->kd', dscore[:, :local_count].astype(jnp.float32), query_h.astype(jnp.float32)) * scale).astype(jnp.bfloat16)
    value_g = jnp.einsum('rk,rd->kd', probs_low[:, :local_count].astype(jnp.float32), grad_h.astype(jnp.float32)).astype(jnp.bfloat16)
    return attn, query_g, key_g, value_g


def reference(queries, keys, values, track, out_weight, grad_out):
    rows = TOK_DEV
    head_dim = D // HEADS
    grad_attn = lax.dot_general(grad_out, out_weight, (((1,), (1,)), ((), ())), preferred_element_type=jnp.float32).astype(jnp.bfloat16)
    per_block = rows // BLOCK

    def split_heads(array):
        return array.reshape(array.shape[0], HEADS, head_dim).transpose(1, 0, 2)

    def one_span(span_id):
        base = span_id * rows
        q_c = lax.dynamic_slice_in_dim(queries, base, rows, 0)
        k_c = lax.dynamic_slice_in_dim(keys, base, rows, 0)
        v_c = lax.dynamic_slice_in_dim(values, base, rows, 0)
        g_c = lax.dynamic_slice_in_dim(grad_attn, base, rows, 0)
        mem_keys = []
        mem_values = []
        for distance in range(1, WINDOW + 1):
            source = jnp.maximum(span_id - distance, 0).astype(jnp.int32) * rows
            mem_keys.append(lax.dynamic_slice_in_dim(keys, source, rows, 0))
            mem_values.append(lax.dynamic_slice_in_dim(values, source, rows, 0))
        all_keys = jnp.concatenate([k_c] + mem_keys, axis=0)
        all_values = jnp.concatenate([v_c] + mem_values, axis=0)
        tracks = lax.dynamic_slice_in_dim(track, (span_id * per_block).astype(jnp.int32), per_block, 0)
        lookback = jnp.arange(WINDOW * per_block, dtype=jnp.int32) // per_block + 1
        block_ok = (tracks == 1) & (lookback[None, :] <= span_id)
        mem_ok = jnp.repeat(jnp.repeat(block_ok, BLOCK, axis=0), BLOCK, axis=1)
        position = jnp.arange(rows, dtype=jnp.int32)
        local_ok = position[:, None] >= position[None, :]
        allowed = jnp.concatenate([local_ok, mem_ok], axis=1)
        fn = jax.vmap(lambda a, b, c, d: head_grads(a, b, c, d, allowed, rows))
        attn, query_g, key_g, value_g = fn(split_heads(q_c), split_heads(all_keys), split_heads(all_values), split_heads(g_c))

        def merge_heads(array):
            return array.transpose(1, 0, 2).reshape(array.shape[1], D)

        return merge_heads(attn), merge_heads(query_g), merge_heads(key_g), merge_heads(value_g)

    attn, query_g, key_g, value_g = lax.map(one_span, jnp.arange(N_SPAN, dtype=jnp.int32))
    attn = attn.reshape(TOKENS, D)
    weight_grad = jnp.dot(attn.T, grad_out, preferred_element_type=jnp.float32)
    return query_g.reshape(TOKENS, D), key_g.reshape(TOKENS, D), value_g.reshape(TOKENS, D), weight_grad
```

```python
import functools

import jax
import jax.numpy as jnp
from jax import lax
from jax.experimental import pallas as pl
from jax.experimental.pallas import tpu as pltpu
from jax.sharding import PartitionSpec as P

HEADS = 16
BLOCK = 128
PLANE = 4
OWN = 8
SLOTS = 9
PAIR = 128
F32 = jnp.float32
BF16 = jnp.bfloat16
MESH = pl.DeviceIdType.MESH
NT = (((1,), (1,)), ((), ()))


def dot(a, b):
    return jnp.dot(a, b, preferred_element_type=F32)


def kernel(
    n, chunks, k_hbm, v_hbm, q_ref, w_ref, go_ref, bias_ref,
    dq_ref, dk_ref, dv_ref, wg_ref,
    kv, kt, vt, s_scr, own_sem, send_sem, recv_sem,
):
    rows = q_ref.shape[0]
    head_dim = PAIR // 2
    scale = head_dim ** (-0.5)
    sid = lax.axis_index("span")
    gid = lax.axis_index("groups")
    i = lax.rem(sid, PLANE)
    z = sid // PLANE
    y = i // 2
    c = lax.rem(i, 2)
    nz = n // PLANE
    yp = sid + 2 - 4 * y
    cp = sid + 1 - 2 * c
    iy = i + 2 - 4 * y
    ic = i + 1 - 2 * c
    iyc = iy + 1 - 2 * c
    up = lax.rem(sid + PLANE, n)
    down = lax.rem(sid + n - PLANE, n)
    has_up = z < nz - 1
    has1 = z >= 1
    has2 = z >= 2

    def own_copy(ch, which):
        src = k_hbm if which == 0 else v_hbm
        cols = pl.ds(pl.multiple_of(ch * PAIR, PAIR), PAIR)
        return pltpu.make_async_copy(src.at[:, cols], kv.at[ch, OWN, which], own_sem.at[ch, which])

    for ch in range(chunks):
        for which in range(2):
            own_copy(ch, which).start()

    def copy(ch, src_slot, dst_slot, target, kind):
        return pltpu.make_async_remote_copy(
            src_ref=kv.at[ch, src_slot],
            dst_ref=kv.at[ch, dst_slot],
            send_sem=send_sem.at[kind, ch],
            recv_sem=recv_sem.at[ch, dst_slot],
            device_id=(gid, target),
            device_id_type=MESH,
        )

    def arrived(ch, slot):
        copy(ch, slot, slot, cp, 0).wait_recv()

    @pl.when(jnp.logical_not(has1))
    def _():
        kv[:, 0:4] = jnp.zeros((chunks, 4, 2, rows, PAIR), BF16)

    for j in range(PLANE):
        @pl.when(jnp.logical_and(jnp.logical_not(has2), i <= j))
        def _():
            kv[:, 4 + j] = jnp.zeros((chunks, 2, rows, PAIR), BF16)

    barrier = pltpu.get_barrier_semaphore()
    for neighbour in (yp, cp):
        pl.semaphore_signal(barrier, inc=1, device_id=(gid, neighbour), device_id_type=MESH)

    @pl.when(has_up)
    def _():
        pl.semaphore_signal(barrier, inc=1, device_id=(gid, up), device_id_type=MESH)

    @pl.when(has1)
    def _():
        pl.semaphore_signal(barrier, inc=1, device_id=(gid, down), device_id_type=MESH)

    pl.semaphore_wait(barrier, 2 + (2 * nz - 2 - z) // nz + (z + nz - 1) // nz)

    relay_z = jnp.logical_and(has1, has_up)
    y1, y0 = y == 1, y == 0
    c1, c0 = c == 1, c == 0

    def stage0(ch):
        own_copy(ch, 0).wait()
        own_copy(ch, 1).wait()

        @pl.when(has_up)
        def _():
            copy(ch, OWN, i, up, 0).start()

        @pl.when(y0)
        def _():
            copy(ch, OWN, 4 + i, yp, 5).start()

        @pl.when(c0)
        def _():
            copy(ch, OWN, 4 + i, cp, 6).start()

    def stage1(ch):
        @pl.when(has1)
        def _():
            arrived(ch, i)

            @pl.when(has_up)
            def _():
                copy(ch, i, 4 + i, up, 1).start()

            copy(ch, i, i, yp, 2).start()
            copy(ch, i, i, cp, 3).start()

        @pl.when(y1)
        def _():
            arrived(ch, 4 + iy)
            copy(ch, 4 + iy, 4 + iy, cp, 7).start()

    def stage2(ch):
        @pl.when(has2)
        def _():
            arrived(ch, 4 + i)

            @pl.when(y1)
            def _():
                copy(ch, 4 + i, 4 + i, yp, 5).start()

            @pl.when(c1)
            def _():
                copy(ch, 4 + i, 4 + i, cp, 6).start()

        @pl.when(has1)
        def _():
            arrived(ch, iy)
            copy(ch, iy, iy, cp, 4).start()

    def stage3(ch):
        @pl.when(jnp.logical_and(y0, has2))
        def _():
            arrived(ch, 4 + iy)
            copy(ch, 4 + iy, 4 + iy, cp, 7).start()

    def stage4(ch):
        @pl.when(has1)
        def _():
            arrived(ch, ic)
            arrived(ch, iyc)

        @pl.when(jnp.logical_or(c1, has2))
        def _():
            arrived(ch, 4 + ic)

        @pl.when(jnp.logical_or(y1, has2))
        def _():
            arrived(ch, 4 + iyc)

    def sent(ch):
        def done(kind):
            copy(ch, OWN, OWN, cp, kind).wait_send()

        @pl.when(has_up)
        def _():
            done(0)

        @pl.when(relay_z)
        def _():
            done(1)

        @pl.when(has1)
        def _():
            done(2)
            done(3)
            done(4)

        @pl.when(jnp.logical_or(y0, has2))
        def _():
            done(5)

        @pl.when(jnp.logical_or(c0, has2))
        def _():
            done(6)

        @pl.when(jnp.logical_or(y1, has2))
        def _():
            done(7)

    def compute(ch):
        cols = pl.ds(pl.multiple_of(ch * PAIR, PAIR), PAIR)
        go = go_ref[...]
        q32 = q_ref[:, cols].astype(F32) * scale
        qs = q32.astype(BF16)
        q_t = q32.T.astype(BF16)
        g_t = lax.dot_general(w_ref[cols, :], go, NT, preferred_element_type=F32).astype(BF16)
        g32_t = g_t.astype(F32)
        g = g32_t.T.astype(BF16)
        head_row = lax.broadcasted_iota(jnp.int32, (PAIR, rows), 0) // head_dim
        head_col = lax.broadcasted_iota(jnp.int32, (rows, PAIR), 1) // head_dim
        causal = lax.broadcasted_iota(jnp.int32, (rows, rows), 0) <= lax.broadcasted_iota(
            jnp.int32, (rows, rows), 1
        )
        for b in range(SLOTS):
            kt[b] = kv[ch, b, 0].T
            vt[b] = kv[ch, b, 1].T
        dk = jnp.zeros((rows, PAIR), F32)
        dv = jnp.zeros((rows, PAIR), F32)
        attn_parts = []
        dq_parts = []
        zero = jnp.zeros((), BF16)
        for h in range(2):
            span = pl.ds(h * head_dim, head_dim)
            q_th = jnp.where(head_row == h, q_t, zero)
            g_th = jnp.where(head_row == h, g_t, zero)
            top = None
            for b in range(SLOTS):
                s = dot(kv[ch, b, 0], q_th)
                if b == OWN:
                    s = jnp.where(causal, s, F32(-1e30))
                else:
                    s = jnp.concatenate(
                        [
                            s[:BLOCK] + bias_ref[2 * b : 2 * b + 1, :],
                            s[BLOCK:] + bias_ref[2 * b + 1 : 2 * b + 2, :],
                        ],
                        axis=0,
                    )
                s_scr[b] = s
                peak = jnp.max(s, axis=0, keepdims=True)
                top = peak if top is None else jnp.maximum(top, peak)
            total = jnp.zeros((1, rows), F32)
            attn = jnp.zeros((head_dim, rows), F32)
            for b in range(SLOTS):
                e = jnp.exp(s_scr[b] - top)
                s_scr[b] = e
                total = total + jnp.sum(e, axis=0, keepdims=True)
                attn = attn + dot(vt[b, span, :], e.astype(BF16))
            inv = 1.0 / total
            attn_low = (attn * inv).astype(BF16)
            delta = jnp.sum(
                g32_t[h * head_dim : (h + 1) * head_dim] * attn_low.astype(F32),
                axis=0,
                keepdims=True,
            )
            dq = jnp.zeros((head_dim, rows), F32)
            for b in range(SLOTS):
                e = s_scr[b]
                ds = e * (dot(kv[ch, b, 1], g_th) - delta)
                dq = dq + dot(kt[b, span, :], ds.astype(BF16))
                if b == OWN:
                    dk = dk + dot(
                        (ds * inv).astype(BF16), jnp.where(head_col == h, qs, zero)
                    )
                    dv = dv + dot((e * inv).astype(BF16), jnp.where(head_col == h, g, zero))
            attn_parts.append(attn_low)
            dq_parts.append(dq * (inv * scale))
        dq_ref[:, cols] = jnp.concatenate(dq_parts, axis=0).T.astype(BF16)
        dk_ref[:, cols] = dk.astype(BF16)
        dv_ref[:, cols] = dv.astype(BF16)
        wg_ref[cols, :] = dot(jnp.concatenate(attn_parts, axis=0), go)

    def step(t, carry):
        for lag, stage in enumerate((stage0, stage1, stage2, stage3)):
            @pl.when(jnp.logical_and(t >= lag, t < chunks + lag))
            def _():
                stage(t - lag)

        @pl.when(t >= 4)
        def _():
            stage4(t - 4)
            compute(t - 4)

        return carry

    lax.fori_loop(0, chunks + 4, step, 0)

    def finish(ch, carry):
        sent(ch)
        return carry

    lax.fori_loop(0, chunks, finish, 0)


def block_bias(track, sid, rows):
    i = lax.rem(sid, PLANE)
    slot = jnp.arange(2 * OWN, dtype=jnp.int32) // 2
    half = jnp.arange(2 * OWN, dtype=jnp.int32) % 2
    gap = i - lax.rem(slot, PLANE)
    look = jnp.where(slot < PLANE, gap + 4, jnp.where(gap > 0, gap, gap + 8))
    column = (look - 1) * 2 + half
    pick = column[:, None] == jnp.arange(track.shape[1], dtype=jnp.int32)[None, :]
    chosen = jnp.sum(jnp.where(pick[None], track[:, None, :], 0), axis=-1)
    ok = (chosen == 1) & (look <= sid)[None, :]
    return jnp.repeat(jnp.where(ok, 0.0, -1e30).astype(F32).T, BLOCK, axis=1)


def shards(n, queries, keys, values, track, out_weight, grad_out):
    rows, width = queries.shape
    chunks = width // PAIR
    sid = lax.axis_index("span")
    bias = block_bias(track, sid, rows)
    grad = jax.ShapeDtypeStruct((rows, width), BF16)
    vmem = pl.BlockSpec(memory_space=pltpu.VMEM)
    dq, dk, dv, wg = pl.pallas_call(
        functools.partial(kernel, n, chunks),
        out_shape=(grad, grad, grad, jax.ShapeDtypeStruct((width, width), F32)),
        in_specs=[pl.BlockSpec(memory_space=pl.ANY)] * 2 + [vmem] * 4,
        out_specs=(vmem,) * 4,
        scratch_shapes=[
            pltpu.VMEM((chunks, SLOTS, 2, rows, PAIR), BF16),
            pltpu.VMEM((SLOTS, PAIR, rows), BF16),
            pltpu.VMEM((SLOTS, PAIR, rows), BF16),
            pltpu.VMEM((SLOTS, rows, rows), F32),
            pltpu.SemaphoreType.DMA((chunks, 2)),
            pltpu.SemaphoreType.DMA((8, chunks)),
            pltpu.SemaphoreType.DMA((chunks, OWN)),
        ],
        compiler_params=pltpu.CompilerParams(
            collective_id=0, has_side_effects=True, vmem_limit_bytes=60 * 1024 * 1024
        ),
    )(keys, values, queries, out_weight, grad_out, bias)
    weight_grad = lax.psum_scatter(wg, "span", scatter_dimension=0, tiled=True)
    return (dq, dk, dv, weight_grad)


def solution(mesh):
    split = P(("groups", "span"), None)
    return jax.shard_map(
        functools.partial(shards, mesh.shape["span"]),
        mesh=mesh,
        in_specs=(split, split, split, split, P(), split),
        out_specs=(split,) * 4,
        check_vma=False,
    )
```

```python
import functools

import jax
import jax.numpy as jnp
from jax import lax
from jax.experimental import pallas as pl
from jax.experimental.pallas import tpu as pltpu
from jax.sharding import PartitionSpec as P

HEADS = 16
BLOCK = 128
PLANE = 4
OWN = 8
SLOTS = 9
PAIR = 128
F32 = jnp.float32
BF16 = jnp.bfloat16
MESH = pl.DeviceIdType.MESH
NT = (((1,), (1,)), ((), ()))


def dot(a, b):
    return jnp.dot(a, b, preferred_element_type=F32)


def kernel(
    n, chunks, k_hbm, v_hbm, q_ref, w_ref, go_ref, bias_ref,
    dq_ref, dk_ref, dv_ref, wg_ref,
    kv, kt, vt, s_scr, own_sem, send_sem, recv_sem, *rs,
):
    rows = q_ref.shape[0]
    head_dim = PAIR // 2
    scale = head_dim ** (-0.5)
    sid = lax.axis_index("span")
    gid = lax.axis_index("groups")
    i = lax.rem(sid, PLANE)
    z = sid // PLANE
    y = i // 2
    c = lax.rem(i, 2)
    nz = n // PLANE
    yp = sid + 2 - 4 * y
    cp = sid + 1 - 2 * c
    iy = i + 2 - 4 * y
    ic = i + 1 - 2 * c
    iyc = iy + 1 - 2 * c
    up = lax.rem(sid + PLANE, n)
    down = lax.rem(sid + n - PLANE, n)
    has_up = z < nz - 1
    has1 = z >= 1
    has2 = z >= 2

    def own_copy(ch, which):
        src = k_hbm if which == 0 else v_hbm
        cols = pl.ds(pl.multiple_of(ch * PAIR, PAIR), PAIR)
        return pltpu.make_async_copy(src.at[:, cols], kv.at[ch, OWN, which], own_sem.at[ch, which])

    for ch in range(chunks):
        for which in range(2):
            own_copy(ch, which).start()

    def copy(ch, src_slot, dst_slot, target, kind):
        return pltpu.make_async_remote_copy(
            src_ref=kv.at[ch, src_slot],
            dst_ref=kv.at[ch, dst_slot],
            send_sem=send_sem.at[kind, ch],
            recv_sem=recv_sem.at[ch, dst_slot],
            device_id=(gid, target),
            device_id_type=MESH,
        )

    def arrived(ch, slot):
        copy(ch, slot, slot, cp, 0).wait_recv()

    @pl.when(jnp.logical_not(has1))
    def _():
        kv[:, 0:4] = jnp.zeros((chunks, 4, 2, rows, PAIR), BF16)

    for j in range(PLANE):
        @pl.when(jnp.logical_and(jnp.logical_not(has2), i <= j))
        def _():
            kv[:, 4 + j] = jnp.zeros((chunks, 2, rows, PAIR), BF16)

    barrier = pltpu.get_barrier_semaphore()
    for neighbour in (yp, cp):
        pl.semaphore_signal(barrier, inc=1, device_id=(gid, neighbour), device_id_type=MESH)
    if rs:
        for other in range(nz):
            @pl.when(z != other)
            def _():
                pl.semaphore_signal(
                    barrier, inc=1, device_id=(gid, PLANE * other + i), device_id_type=MESH
                )

        pl.semaphore_wait(barrier, 1 + nz)
    else:
        @pl.when(has_up)
        def _():
            pl.semaphore_signal(barrier, inc=1, device_id=(gid, up), device_id_type=MESH)

        @pl.when(has1)
        def _():
            pl.semaphore_signal(barrier, inc=1, device_id=(gid, down), device_id_type=MESH)

        pl.semaphore_wait(barrier, 2 + (2 * nz - 2 - z) // nz + (z + nz - 1) // nz)

    relay_z = jnp.logical_and(has1, has_up)
    y1, y0 = y == 1, y == 0
    c1, c0 = c == 1, c == 0

    def stage0(ch):
        own_copy(ch, 0).wait()
        own_copy(ch, 1).wait()

        @pl.when(has_up)
        def _():
            copy(ch, OWN, i, up, 0).start()

        @pl.when(y0)
        def _():
            copy(ch, OWN, 4 + i, yp, 5).start()

        @pl.when(c0)
        def _():
            copy(ch, OWN, 4 + i, cp, 6).start()

    def stage1(ch):
        @pl.when(has1)
        def _():
            arrived(ch, i)

            @pl.when(has_up)
            def _():
                copy(ch, i, 4 + i, up, 1).start()

            copy(ch, i, i, yp, 2).start()
            copy(ch, i, i, cp, 3).start()

        @pl.when(y1)
        def _():
            arrived(ch, 4 + iy)
            copy(ch, 4 + iy, 4 + iy, cp, 7).start()

    def stage2(ch):
        @pl.when(has2)
        def _():
            arrived(ch, 4 + i)

            @pl.when(y1)
            def _():
                copy(ch, 4 + i, 4 + i, yp, 5).start()

            @pl.when(c1)
            def _():
                copy(ch, 4 + i, 4 + i, cp, 6).start()

        @pl.when(has1)
        def _():
            arrived(ch, iy)
            copy(ch, iy, iy, cp, 4).start()

    def stage3(ch):
        @pl.when(jnp.logical_and(y0, has2))
        def _():
            arrived(ch, 4 + iy)
            copy(ch, 4 + iy, 4 + iy, cp, 7).start()

    def stage4(ch):
        @pl.when(has1)
        def _():
            arrived(ch, ic)
            arrived(ch, iyc)

        @pl.when(jnp.logical_or(c1, has2))
        def _():
            arrived(ch, 4 + ic)

        @pl.when(jnp.logical_or(y1, has2))
        def _():
            arrived(ch, 4 + iyc)

    def sent(ch):
        def done(kind):
            copy(ch, OWN, OWN, cp, kind).wait_send()

        @pl.when(has_up)
        def _():
            done(0)

        @pl.when(relay_z)
        def _():
            done(1)

        @pl.when(has1)
        def _():
            done(2)
            done(3)
            done(4)

        @pl.when(jnp.logical_or(y0, has2))
        def _():
            done(5)

        @pl.when(jnp.logical_or(c0, has2))
        def _():
            done(6)

        @pl.when(jnp.logical_or(y1, has2))
        def _():
            done(7)

    if rs:
        heads, mine, src0, dst0, src1, dst1, src2, dst2, rs_send, rs_recv, z_recv = rs

    def core_copy(ch):
        return pltpu.make_async_remote_copy(
            src_ref=src0.at[ch], dst_ref=dst0.at[ch],
            send_sem=rs_send.at[0, ch], recv_sem=rs_recv.at[0, ch],
            device_id=(gid, cp), device_id_type=MESH,
        )

    def y_copy(ch):
        return pltpu.make_async_remote_copy(
            src_ref=src1.at[ch], dst_ref=dst1.at[ch],
            send_sem=rs_send.at[1, ch], recv_sem=rs_recv.at[1, ch],
            device_id=(gid, yp), device_id_type=MESH,
        )

    def z_copy(ch, slot):
        return pltpu.make_async_remote_copy(
            src_ref=src2.at[ch], dst_ref=dst2.at[slot],
            send_sem=rs_send.at[2, ch], recv_sem=z_recv.at[slot],
            device_id=(gid, PLANE * (ch // 2) + i), device_id_type=MESH,
        )

    def reduce_core(ch, go):
        mine[ch] = dot(heads[c], go)
        src0[ch] = dot(heads[1 - c], go).astype(BF16)
        core_copy(ch).start()

    def reduce_y(ch):
        core_copy(ch).wait_recv()
        part = mine[ch] + dst0[ch].astype(F32)

        @pl.when(y != lax.rem(ch, 2))
        def _():
            src1[ch] = part.astype(BF16)
            y_copy(ch).start()

        @pl.when(y == lax.rem(ch, 2))
        def _():
            mine[ch] = part

    def reduce_z(ch):
        @pl.when(y == lax.rem(ch, 2))
        def _():
            y_copy(ch).wait_recv()
            part = mine[ch] + dst1[ch].astype(F32)

            @pl.when(z != ch // 2)
            def _():
                src2[ch] = part.astype(BF16)
                z_copy(ch, z).start()

            @pl.when(z == ch // 2)
            def _():
                wg_ref[...] = part

    def reduce_end():
        for other in range(nz):
            @pl.when(z != other)
            def _():
                pltpu.make_async_remote_copy(
                    src_ref=src2.at[0], dst_ref=dst2.at[other],
                    send_sem=rs_send.at[2, 0], recv_sem=z_recv.at[other],
                    device_id=(gid, yp), device_id_type=MESH,
                ).wait_recv()
                wg_ref[...] += dst2[other].astype(F32)

    def reduce_sent(ch):
        core_copy(ch).wait_send()

        @pl.when(y != lax.rem(ch, 2))
        def _():
            y_copy(ch).wait_send()

        @pl.when(jnp.logical_and(y == lax.rem(ch, 2), z != ch // 2))
        def _():
            pltpu.make_async_remote_copy(
                src_ref=src2.at[ch], dst_ref=dst2.at[z],
                send_sem=rs_send.at[2, ch], recv_sem=z_recv.at[z],
                device_id=(gid, yp), device_id_type=MESH,
            ).wait_send()

    def compute(ch):
        cols = pl.ds(pl.multiple_of(ch * PAIR, PAIR), PAIR)
        go = go_ref[...]
        q32 = q_ref[:, cols].astype(F32) * scale
        qs = q32.astype(BF16)
        q_t = q32.T.astype(BF16)
        g_t = lax.dot_general(w_ref[cols, :], go, NT, preferred_element_type=F32).astype(BF16)
        g32_t = g_t.astype(F32)
        g = g32_t.T.astype(BF16)
        head_row = lax.broadcasted_iota(jnp.int32, (PAIR, rows), 0) // head_dim
        head_col = lax.broadcasted_iota(jnp.int32, (rows, PAIR), 1) // head_dim
        causal = lax.broadcasted_iota(jnp.int32, (rows, rows), 0) <= lax.broadcasted_iota(
            jnp.int32, (rows, rows), 1
        )
        for b in range(SLOTS):
            kt[b] = kv[ch, b, 0].T
            vt[b] = kv[ch, b, 1].T
        zero = jnp.zeros((), BF16)
        stats = []
        for h in range(2):
            span = pl.ds(h * head_dim, head_dim)
            q_th = jnp.where(head_row == h, q_t, zero)
            top = None
            for b in range(SLOTS):
                s = dot(kv[ch, b, 0], q_th)
                if b == OWN:
                    s = jnp.where(causal, s, F32(-1e30))
                else:
                    s = jnp.concatenate(
                        [
                            s[:BLOCK] + bias_ref[2 * b : 2 * b + 1, :],
                            s[BLOCK:] + bias_ref[2 * b + 1 : 2 * b + 2, :],
                        ],
                        axis=0,
                    )
                s_scr[h, b] = s
                peak = jnp.max(s, axis=0, keepdims=True)
                top = peak if top is None else jnp.maximum(top, peak)
            total = jnp.zeros((1, rows), F32)
            attn = jnp.zeros((head_dim, rows), F32)
            for b in range(SLOTS):
                e = jnp.exp(s_scr[h, b] - top)
                s_scr[h, b] = e
                total = total + jnp.sum(e, axis=0, keepdims=True)
                attn = attn + dot(vt[b, span, :], e.astype(BF16))
            inv = 1.0 / total
            attn_low = (attn * inv).astype(BF16)
            delta = jnp.sum(
                g32_t[h * head_dim : (h + 1) * head_dim] * attn_low.astype(F32),
                axis=0,
                keepdims=True,
            )
            stats.append((inv, delta, attn_low))
            if rs:
                heads[h] = attn_low
        if rs:
            reduce_core(ch, go)
        else:
            wg_ref[cols, :] = dot(jnp.concatenate([s[2] for s in stats], axis=0), go)
        dk = jnp.zeros((rows, PAIR), F32)
        dv = jnp.zeros((rows, PAIR), F32)
        dq_parts = []
        for h in range(2):
            span = pl.ds(h * head_dim, head_dim)
            inv, delta, _ = stats[h]
            g_th = jnp.where(head_row == h, g_t, zero)
            dq = jnp.zeros((head_dim, rows), F32)
            for b in range(SLOTS):
                e = s_scr[h, b]
                ds = e * (dot(kv[ch, b, 1], g_th) - delta)
                dq = dq + dot(kt[b, span, :], ds.astype(BF16))
                if b == OWN:
                    dk = dk + dot(
                        (ds * inv).astype(BF16), jnp.where(head_col == h, qs, zero)
                    )
                    dv = dv + dot((e * inv).astype(BF16), jnp.where(head_col == h, g, zero))
            dq_parts.append(dq * (inv * scale))
        dq_ref[:, cols] = jnp.concatenate(dq_parts, axis=0).T.astype(BF16)
        dk_ref[:, cols] = dk.astype(BF16)
        dv_ref[:, cols] = dv.astype(BF16)

    def step(t, carry):
        for lag, stage in enumerate((stage0, stage1, stage2, stage3)):
            @pl.when(jnp.logical_and(t >= lag, t < chunks + lag))
            def _():
                stage(t - lag)

        @pl.when(t >= 4)
        def _():
            stage4(t - 4)
            if rs:
                @pl.when(t >= 5)
                def _():
                    reduce_z(t - 5)

            compute(t - 4)
            if rs:
                reduce_y(t - 4)

        return carry

    lax.fori_loop(0, chunks + 4, step, 0)

    if rs:
        reduce_z(chunks - 1)
        reduce_end()

    def finish(ch, carry):
        sent(ch)
        if rs:
            reduce_sent(ch)
        return carry

    lax.fori_loop(0, chunks, finish, 0)


def block_bias(track, sid, rows):
    i = lax.rem(sid, PLANE)
    slot = jnp.arange(2 * OWN, dtype=jnp.int32) // 2
    half = jnp.arange(2 * OWN, dtype=jnp.int32) % 2
    gap = i - lax.rem(slot, PLANE)
    look = jnp.where(slot < PLANE, gap + 4, jnp.where(gap > 0, gap, gap + 8))
    column = (look - 1) * 2 + half
    pick = column[:, None] == jnp.arange(track.shape[1], dtype=jnp.int32)[None, :]
    chosen = jnp.sum(jnp.where(pick[None], track[:, None, :], 0), axis=-1)
    ok = (chosen == 1) & (look <= sid)[None, :]
    return jnp.repeat(jnp.where(ok, 0.0, -1e30).astype(F32).T, BLOCK, axis=1)


def shards(n, queries, keys, values, track, out_weight, grad_out):
    rows, width = queries.shape
    chunks = width // PAIR
    sid = lax.axis_index("span")
    bias = block_bias(track, sid, rows)
    share = width // n
    inside = 2 * share == PAIR and n % PLANE == 0
    grad = jax.ShapeDtypeStruct((rows, width), BF16)
    wg_rows = share if inside else width
    term = (share, width)
    rs = [
        pltpu.VMEM((2, share, rows), BF16),
        pltpu.VMEM((chunks, *term), F32),
        *[pltpu.VMEM((chunks, *term), BF16)] * 5,
        pltpu.VMEM((n // PLANE, *term), BF16),
        pltpu.SemaphoreType.DMA((3, chunks)),
        pltpu.SemaphoreType.DMA((2, chunks)),
        pltpu.SemaphoreType.DMA((n // PLANE,)),
    ]
    vmem = pl.BlockSpec(memory_space=pltpu.VMEM)
    dq, dk, dv, wg = pl.pallas_call(
        functools.partial(kernel, n, chunks),
        out_shape=(grad, grad, grad, jax.ShapeDtypeStruct((wg_rows, width), F32)),
        in_specs=[pl.BlockSpec(memory_space=pl.ANY)] * 2 + [vmem] * 4,
        out_specs=(vmem,) * 4,
        scratch_shapes=[
            pltpu.VMEM((chunks, SLOTS, 2, rows, PAIR), BF16),
            pltpu.VMEM((SLOTS, PAIR, rows), BF16),
            pltpu.VMEM((SLOTS, PAIR, rows), BF16),
            pltpu.VMEM((2, SLOTS, rows, rows), F32),
            pltpu.SemaphoreType.DMA((chunks, 2)),
            pltpu.SemaphoreType.DMA((8, chunks)),
            pltpu.SemaphoreType.DMA((chunks, OWN)),
        ] + (rs if inside else []),
        compiler_params=pltpu.CompilerParams(
            collective_id=0, has_side_effects=True, vmem_limit_bytes=60 * 1024 * 1024
        ),
    )(keys, values, queries, out_weight, grad_out, bias)
    if not inside:
        wg = lax.psum_scatter(wg, "span", scatter_dimension=0, tiled=True)
    return (dq, dk, dv, wg)


def solution(mesh):
    split = P(("groups", "span"), None)
    return jax.shard_map(
        functools.partial(shards, mesh.shape["span"]),
        mesh=mesh,
        in_specs=(split, split, split, split, P(), split),
        out_specs=(split,) * 4,
        check_vma=False,
    )
```

```python
import functools

import jax
import jax.numpy as jnp
from jax import lax
from jax.experimental import pallas as pl
from jax.experimental.pallas import tpu as pltpu
from jax.sharding import PartitionSpec as P

HEADS = 16
BLOCK = 128
PLANE = 4
OWN = 8
SLOTS = 9
PAIR = 128
F32 = jnp.float32
BF16 = jnp.bfloat16
MESH = pl.DeviceIdType.MESH
NT = (((1,), (1,)), ((), ()))


def dot(a, b):
    return jnp.dot(a, b, preferred_element_type=F32)


def kernel(
    n, chunks, k_hbm, v_hbm, q_ref, w_ref, go_ref, bias_ref,
    dq_ref, dk_ref, dv_ref, wg_ref,
    kv, kt, vt, s_scr, own_sem, send_sem, recv_sem, *rs,
):
    rows = q_ref.shape[0]
    head_dim = PAIR // 2
    scale = head_dim ** (-0.5)
    sid = lax.axis_index("span")
    gid = lax.axis_index("groups")
    i = lax.rem(sid, PLANE)
    z = sid // PLANE
    y = i // 2
    c = lax.rem(i, 2)
    nz = n // PLANE
    yp = sid + 2 - 4 * y
    cp = sid + 1 - 2 * c
    iy = i + 2 - 4 * y
    ic = i + 1 - 2 * c
    iyc = iy + 1 - 2 * c
    up = lax.rem(sid + PLANE, n)
    down = lax.rem(sid + n - PLANE, n)
    has_up = z < nz - 1
    has1 = z >= 1
    has2 = z >= 2

    def own_copy(ch, which):
        src = k_hbm if which == 0 else v_hbm
        cols = pl.ds(pl.multiple_of(ch * PAIR, PAIR), PAIR)
        return pltpu.make_async_copy(src.at[:, cols], kv.at[ch, OWN, which], own_sem.at[ch, which])

    for ch in range(chunks):
        for which in range(2):
            own_copy(ch, which).start()

    def copy(ch, src_slot, dst_slot, target, kind):
        return pltpu.make_async_remote_copy(
            src_ref=kv.at[ch, src_slot],
            dst_ref=kv.at[ch, dst_slot],
            send_sem=send_sem.at[kind, ch],
            recv_sem=recv_sem.at[ch, dst_slot],
            device_id=(gid, target),
            device_id_type=MESH,
        )

    def arrived(ch, slot):
        copy(ch, slot, slot, cp, 0).wait_recv()

    @pl.when(jnp.logical_not(has1))
    def _():
        kv[:, 0:4] = jnp.zeros((chunks, 4, 2, rows, PAIR), BF16)

    for j in range(PLANE):
        @pl.when(jnp.logical_and(jnp.logical_not(has2), i <= j))
        def _():
            kv[:, 4 + j] = jnp.zeros((chunks, 2, rows, PAIR), BF16)

    barrier = pltpu.get_barrier_semaphore()
    for neighbour in (yp, cp):
        pl.semaphore_signal(barrier, inc=1, device_id=(gid, neighbour), device_id_type=MESH)
    if rs:
        for other in range(nz):
            @pl.when(z != other)
            def _():
                pl.semaphore_signal(
                    barrier, inc=1, device_id=(gid, PLANE * other + i), device_id_type=MESH
                )

        pl.semaphore_wait(barrier, 1 + nz)
    else:
        @pl.when(has_up)
        def _():
            pl.semaphore_signal(barrier, inc=1, device_id=(gid, up), device_id_type=MESH)

        @pl.when(has1)
        def _():
            pl.semaphore_signal(barrier, inc=1, device_id=(gid, down), device_id_type=MESH)

        pl.semaphore_wait(barrier, 2 + (2 * nz - 2 - z) // nz + (z + nz - 1) // nz)

    relay_z = jnp.logical_and(has1, has_up)
    y1, y0 = y == 1, y == 0
    c1, c0 = c == 1, c == 0

    def stage0(ch):
        own_copy(ch, 0).wait()
        own_copy(ch, 1).wait()

        @pl.when(has_up)
        def _():
            copy(ch, OWN, i, up, 0).start()

        @pl.when(y0)
        def _():
            copy(ch, OWN, 4 + i, yp, 5).start()

        @pl.when(c0)
        def _():
            copy(ch, OWN, 4 + i, cp, 6).start()

    def stage1(ch):
        @pl.when(has1)
        def _():
            arrived(ch, i)

            @pl.when(has_up)
            def _():
                copy(ch, i, 4 + i, up, 1).start()

            copy(ch, i, i, yp, 2).start()
            copy(ch, i, i, cp, 3).start()

        @pl.when(y1)
        def _():
            arrived(ch, 4 + iy)
            copy(ch, 4 + iy, 4 + iy, cp, 7).start()

    def stage2(ch):
        @pl.when(has2)
        def _():
            arrived(ch, 4 + i)

            @pl.when(y1)
            def _():
                copy(ch, 4 + i, 4 + i, yp, 5).start()

            @pl.when(c1)
            def _():
                copy(ch, 4 + i, 4 + i, cp, 6).start()

        @pl.when(has1)
        def _():
            arrived(ch, iy)
            copy(ch, iy, iy, cp, 4).start()

    def stage3(ch):
        @pl.when(jnp.logical_and(y0, has2))
        def _():
            arrived(ch, 4 + iy)
            copy(ch, 4 + iy, 4 + iy, cp, 7).start()

    def stage4(ch):
        @pl.when(has1)
        def _():
            arrived(ch, ic)
            arrived(ch, iyc)

        @pl.when(jnp.logical_or(c1, has2))
        def _():
            arrived(ch, 4 + ic)

        @pl.when(jnp.logical_or(y1, has2))
        def _():
            arrived(ch, 4 + iyc)

    def sent(ch):
        def done(kind):
            copy(ch, OWN, OWN, cp, kind).wait_send()

        @pl.when(has_up)
        def _():
            done(0)

        @pl.when(relay_z)
        def _():
            done(1)

        @pl.when(has1)
        def _():
            done(2)
            done(3)
            done(4)

        @pl.when(jnp.logical_or(y0, has2))
        def _():
            done(5)

        @pl.when(jnp.logical_or(c0, has2))
        def _():
            done(6)

        @pl.when(jnp.logical_or(y1, has2))
        def _():
            done(7)

    if rs:
        heads, mine, src0, dst0, src1, dst1, src2, dst2, rs_send, rs_recv, z_recv = rs

    def core_copy(ch):
        return pltpu.make_async_remote_copy(
            src_ref=src0.at[ch], dst_ref=dst0.at[ch],
            send_sem=rs_send.at[0, ch], recv_sem=rs_recv.at[0, ch],
            device_id=(gid, cp), device_id_type=MESH,
        )

    def y_copy(ch):
        return pltpu.make_async_remote_copy(
            src_ref=src1.at[ch], dst_ref=dst1.at[ch],
            send_sem=rs_send.at[1, ch], recv_sem=rs_recv.at[1, ch],
            device_id=(gid, yp), device_id_type=MESH,
        )

    def z_copy(ch, slot):
        return pltpu.make_async_remote_copy(
            src_ref=src2.at[ch], dst_ref=dst2.at[slot],
            send_sem=rs_send.at[2, ch], recv_sem=z_recv.at[slot],
            device_id=(gid, PLANE * (ch // 2) + i), device_id_type=MESH,
        )

    def reduce_core(ch, go):
        mine[ch] = dot(heads[c], go)
        src0[ch] = dot(heads[1 - c], go).astype(BF16)
        core_copy(ch).start()

    def reduce_y(ch):
        core_copy(ch).wait_recv()
        part = mine[ch] + dst0[ch].astype(F32)

        @pl.when(y != lax.rem(ch, 2))
        def _():
            src1[ch] = part.astype(BF16)
            y_copy(ch).start()

        @pl.when(y == lax.rem(ch, 2))
        def _():
            mine[ch] = part

    def reduce_z(ch):
        @pl.when(y == lax.rem(ch, 2))
        def _():
            y_copy(ch).wait_recv()
            part = mine[ch] + dst1[ch].astype(F32)

            @pl.when(z != ch // 2)
            def _():
                src2[ch] = part.astype(BF16)
                z_copy(ch, z).start()

            @pl.when(z == ch // 2)
            def _():
                wg_ref[...] = part

    def reduce_end():
        for other in range(nz):
            @pl.when(z != other)
            def _():
                pltpu.make_async_remote_copy(
                    src_ref=src2.at[0], dst_ref=dst2.at[other],
                    send_sem=rs_send.at[2, 0], recv_sem=z_recv.at[other],
                    device_id=(gid, yp), device_id_type=MESH,
                ).wait_recv()
                wg_ref[...] += dst2[other].astype(F32)

    def reduce_sent(ch):
        core_copy(ch).wait_send()

        @pl.when(y != lax.rem(ch, 2))
        def _():
            y_copy(ch).wait_send()

        @pl.when(jnp.logical_and(y == lax.rem(ch, 2), z != ch // 2))
        def _():
            pltpu.make_async_remote_copy(
                src_ref=src2.at[ch], dst_ref=dst2.at[z],
                send_sem=rs_send.at[2, ch], recv_sem=z_recv.at[z],
                device_id=(gid, yp), device_id_type=MESH,
            ).wait_send()

    def compute(ch):
        cols = pl.ds(pl.multiple_of(ch * PAIR, PAIR), PAIR)
        go = go_ref[...]
        q32 = q_ref[:, cols].astype(F32) * scale
        qs = q32.astype(BF16)
        q_t = q32.T.astype(BF16)
        g_t = lax.dot_general(w_ref[cols, :], go, NT, preferred_element_type=F32).astype(BF16)
        g32_t = g_t.astype(F32)
        g = g32_t.T.astype(BF16)
        head_row = lax.broadcasted_iota(jnp.int32, (PAIR, rows), 0) // head_dim
        head_col = lax.broadcasted_iota(jnp.int32, (rows, PAIR), 1) // head_dim
        causal = lax.broadcasted_iota(jnp.int32, (rows, rows), 0) <= lax.broadcasted_iota(
            jnp.int32, (rows, rows), 1
        )
        for b in range(SLOTS):
            kt[b] = kv[ch, b, 0].T
            vt[b] = kv[ch, b, 1].T
        zero = jnp.zeros((), BF16)
        stats = []
        for h in range(2):
            span = pl.ds(h * head_dim, head_dim)
            q_th = jnp.where(head_row == h, q_t, zero)
            top = None
            for b in range(SLOTS):
                s = dot(kv[ch, b, 0], q_th)
                if b == OWN:
                    s = jnp.where(causal, s, F32(-1e30))
                else:
                    s = jnp.concatenate(
                        [
                            s[:BLOCK] + bias_ref[2 * b : 2 * b + 1, :],
                            s[BLOCK:] + bias_ref[2 * b + 1 : 2 * b + 2, :],
                        ],
                        axis=0,
                    )
                s_scr[h, b] = s
                peak = jnp.max(s, axis=0, keepdims=True)
                top = peak if top is None else jnp.maximum(top, peak)
            total = jnp.zeros((1, rows), F32)
            attn = jnp.zeros((head_dim, rows), F32)
            for b in range(SLOTS):
                e = jnp.exp(s_scr[h, b] - top)
                s_scr[h, b] = e
                total = total + jnp.sum(e, axis=0, keepdims=True)
                attn = attn + dot(vt[b, span, :], e.astype(BF16))
            inv = 1.0 / total
            attn_low = (attn * inv).astype(BF16)
            delta = jnp.sum(
                g32_t[h * head_dim : (h + 1) * head_dim] * attn_low.astype(F32),
                axis=0,
                keepdims=True,
            )
            stats.append((inv, delta, attn_low))
            if rs:
                heads[h] = attn_low
        if rs:
            reduce_core(ch, go)
        else:
            wg_ref[cols, :] = dot(jnp.concatenate([s[2] for s in stats], axis=0), go)
        dk = jnp.zeros((rows, PAIR), F32)
        dv = jnp.zeros((rows, PAIR), F32)
        dq_parts = []
        for h in range(2):
            span = pl.ds(h * head_dim, head_dim)
            inv, delta, _ = stats[h]
            g_th = jnp.where(head_row == h, g_t, zero)
            dq = jnp.zeros((head_dim, rows), F32)
            for b in range(SLOTS):
                e = s_scr[h, b]
                ds = e * (dot(kv[ch, b, 1], g_th) - delta)
                dq = dq + dot(kt[b, span, :], ds.astype(BF16))
                if b == OWN:
                    dk = dk + dot(
                        (ds * inv).astype(BF16), jnp.where(head_col == h, qs, zero)
                    )
                    dv = dv + dot((e * inv).astype(BF16), jnp.where(head_col == h, g, zero))
            dq_parts.append(dq * (inv * scale))
        dq_ref[:, cols] = jnp.concatenate(dq_parts, axis=0).T.astype(BF16)
        dk_ref[:, cols] = dk.astype(BF16)
        dv_ref[:, cols] = dv.astype(BF16)

    def step(t, carry):
        for lag, stage in enumerate((stage0, stage1, stage2, stage3)):
            @pl.when(jnp.logical_and(t >= lag, t < chunks + lag))
            def _():
                stage(t - lag)

        @pl.when(t >= 4)
        def _():
            stage4(t - 4)
            compute(t - 4)

        if rs:
            for k, (ys, zs) in enumerate(((3, 0), (5, 3), (6, 5), (7, 6))):
                y_from = (0, 3, 5, 6)[k]
                z_from = (0, 0, 3, 5)[k]

                @pl.when(t == chunks + k)
                def _():
                    for ch in range(y_from, ys):
                        reduce_y(ch)
                    for ch in range(z_from, zs):
                        reduce_z(ch)

        return carry

    lax.fori_loop(0, chunks + 4, step, 0)

    if rs:
        reduce_y(chunks - 1)
        reduce_z(chunks - 2)
        reduce_z(chunks - 1)
        reduce_end()

    def finish(ch, carry):
        sent(ch)
        if rs:
            reduce_sent(ch)
        return carry

    lax.fori_loop(0, chunks, finish, 0)


def block_bias(track, sid, rows):
    i = lax.rem(sid, PLANE)
    slot = jnp.arange(2 * OWN, dtype=jnp.int32) // 2
    half = jnp.arange(2 * OWN, dtype=jnp.int32) % 2
    gap = i - lax.rem(slot, PLANE)
    look = jnp.where(slot < PLANE, gap + 4, jnp.where(gap > 0, gap, gap + 8))
    column = (look - 1) * 2 + half
    pick = column[:, None] == jnp.arange(track.shape[1], dtype=jnp.int32)[None, :]
    chosen = jnp.sum(jnp.where(pick[None], track[:, None, :], 0), axis=-1)
    ok = (chosen == 1) & (look <= sid)[None, :]
    return jnp.repeat(jnp.where(ok, 0.0, -1e30).astype(F32).T, BLOCK, axis=1)


def shards(n, queries, keys, values, track, out_weight, grad_out):
    rows, width = queries.shape
    chunks = width // PAIR
    sid = lax.axis_index("span")
    bias = block_bias(track, sid, rows)
    share = width // n
    inside = 2 * share == PAIR and n % PLANE == 0
    grad = jax.ShapeDtypeStruct((rows, width), BF16)
    wg_rows = share if inside else width
    term = (share, width)
    rs = [
        pltpu.VMEM((2, share, rows), BF16),
        pltpu.VMEM((chunks, *term), F32),
        *[pltpu.VMEM((chunks, *term), BF16)] * 5,
        pltpu.VMEM((n // PLANE, *term), BF16),
        pltpu.SemaphoreType.DMA((3, chunks)),
        pltpu.SemaphoreType.DMA((2, chunks)),
        pltpu.SemaphoreType.DMA((n // PLANE,)),
    ]
    vmem = pl.BlockSpec(memory_space=pltpu.VMEM)
    dq, dk, dv, wg = pl.pallas_call(
        functools.partial(kernel, n, chunks),
        out_shape=(grad, grad, grad, jax.ShapeDtypeStruct((wg_rows, width), F32)),
        in_specs=[pl.BlockSpec(memory_space=pl.ANY)] * 2 + [vmem] * 4,
        out_specs=(vmem,) * 4,
        scratch_shapes=[
            pltpu.VMEM((chunks, SLOTS, 2, rows, PAIR), BF16),
            pltpu.VMEM((SLOTS, PAIR, rows), BF16),
            pltpu.VMEM((SLOTS, PAIR, rows), BF16),
            pltpu.VMEM((2, SLOTS, rows, rows), F32),
            pltpu.SemaphoreType.DMA((chunks, 2)),
            pltpu.SemaphoreType.DMA((8, chunks)),
            pltpu.SemaphoreType.DMA((chunks, OWN)),
        ] + (rs if inside else []),
        compiler_params=pltpu.CompilerParams(
            collective_id=0, has_side_effects=True, vmem_limit_bytes=36 * 1024 * 1024
        ),
    )(keys, values, queries, out_weight, grad_out, bias)
    if not inside:
        wg = lax.psum_scatter(wg, "span", scatter_dimension=0, tiled=True)
    return (dq, dk, dv, wg)


def solution(mesh):
    split = P(("groups", "span"), None)
    return jax.shard_map(
        functools.partial(shards, mesh.shape["span"]),
        mesh=mesh,
        in_specs=(split, split, split, split, P(), split),
        out_specs=(split,) * 4,
        check_vma=False,
    )
```
